512 devices in a mesh: seq: 128 (over x, z_lo, y, core), head: 4 (over z_hi).
Axes of the slice: x: 4, y: 4, z: 16 (z_hi: 4, z_lo: 4; z = z_hi * 4 + z_lo), core: 2. Of those that a mesh axis runs over, the one named last changes fastest.
Arguments:
- query_rows: bfloat16 [65536, 2048], P('seq', 'head'), may hold values from -18 to 18
- key_rows: bfloat16 [65536, 2048], P('seq', 'head'), may hold values from -18 to 18
- value_rows: bfloat16 [65536, 2048], P('seq', 'head'), may hold values from -6 to 6
- out_grad: bfloat16 [65536, 4096], P('seq', 'head'), may hold values from -6 to 6
- out_weight: bfloat16 [2048, 4096], P('head', 'seq'), may hold values from -0.09375 to 0.09375
Outputs:
- attended: bfloat16 [65536, 2048], P('seq', 'head')
- query_grad: bfloat16 [65536, 2048], P('seq', 'head')
- key_grad: bfloat16 [65536, 2048], P('seq', 'head')
- value_grad: bfloat16 [65536, 2048], P('seq', 'head')
The draws below stay inside these ranges and needn't reach their ends.
All inputs are finite; a program needn't handle non-finite values.
Results may differ from the reference program's by a relative error of at most 0.0067.
Values may be sent and summed in bfloat16 or wider, within the bound.
No kernel may reach another device: no remote copies, remote signals or barrier semaphores. Data moves between devices by JAX's collectives and lax.ppermute only.
A program may use at most 64 MiB of HBM per device.

```python
import jax
import jax.numpy as jnp
from jax import lax

D = 4096
HEADS = 16
DH = 128
STRIDE = 512
BLOCK = 128
TOKENS = 65536
N_SEQ = 128


def base_values(key):
    return jnp.clip(jax.random.normal(key, (TOKENS, HEADS * DH), jnp.float32), -6.0, 6.0)


def draw_query_rows(key, part):
    values = base_values(jax.random.fold_in(key, 1))
    return values.astype(jnp.bfloat16)


def draw_key_rows(key, part):
    values = base_values(jax.random.fold_in(key, 2))
    return values.astype(jnp.bfloat16)


def shard_levels(key, extent, cuts, least, largest):
    gain = 1.0
    for axis_at, blocks in cuts:
        heights = jax.random.uniform(jax.random.fold_in(jax.random.fold_in(key, 6), axis_at), (blocks,), jnp.float32, least / len(cuts), largest / len(cuts))
        gain = gain * jnp.repeat(jnp.exp(heights), extent[axis_at] // blocks).reshape((-1,) + (1,) * (len(extent) - 1 - axis_at))
    return gain


def gaussian(key, dims, width, reach, cuts=(), kind=jnp.bfloat16):
    array = jax.random.normal(key, dims, jnp.float32) * width
    if len(cuts) > 0:
        array = shard_levels(key, dims, cuts, -0.22, 0.18) * array
    return jnp.clip(array, min=-reach, max=reach).astype(kind)


def setup_inputs(seed: int = 0) -> dict:
    splits = jax.random.split(jax.random.key(seed), 6)
    query_rows = draw_query_rows(jax.random.fold_in(splits[5], 71), 0)
    key_rows = draw_key_rows(jax.random.fold_in(splits[5], 71), 0)
    value_rows = gaussian(splits[2], (TOKENS, HEADS * DH), 1.0, 6.0, ((0, 128), (1, 4)))
    out_grad = gaussian(splits[3], (TOKENS, D), 1.0, 6.0, ((0, 128), (1, 4)))
    out_weight = gaussian(splits[4], (HEADS * DH, D), D ** -0.5, 0.09375, ((0, 4), (1, 128)))
    return {"query_rows": query_rows, "key_rows": key_rows, "value_rows": value_rows, "out_grad": out_grad, "out_weight": out_weight}


SENTINEL = -1.0e30


def rounded(values):
    return lax.optimization_barrier(values.astype(jnp.bfloat16)).astype(jnp.float32)


def part_forward(queries, keys_part, values_part, visible, layout_forms):
    query_form, key_form, score_form = layout_forms
    scaling = DH ** -0.5
    scores = jnp.einsum(query_form + "," + key_form + "->" + score_form, queries.astype(jnp.float32), keys_part.astype(jnp.float32)) * scaling
    row_max = jnp.max(jnp.where(visible, scores, SENTINEL), axis=-1)
    weights = jnp.where(visible, jnp.exp(scores - row_max[..., None]), 0.0)
    row_sum = jnp.sum(weights, axis=-1)
    partial_out = jnp.einsum(score_form + "," + key_form + "->" + query_form, rounded(weights), values_part.astype(jnp.float32))
    return scores, row_max, row_sum, partial_out


def part_backward(scores, visible, lse_rows, delta_rows, queries, keys_part, values_part, grad_part, layout_forms):
    query_form, key_form, score_form = layout_forms
    scaling = DH ** -0.5
    probs = jnp.where(visible, jnp.exp(scores - lse_rows[..., None]), 0.0)
    value_part_grad = jnp.einsum(score_form + "," + query_form + "->" + key_form, rounded(probs), grad_part.astype(jnp.float32))
    dprob = jnp.einsum(query_form + "," + key_form + "->" + score_form, grad_part.astype(jnp.float32), values_part.astype(jnp.float32))
    dscore = rounded(probs * (dprob - delta_rows[..., None]))
    query_part_grad = jnp.einsum(score_form + "," + key_form + "->" + query_form, dscore, keys_part.astype(jnp.float32)) * scaling
    key_part_grad = jnp.einsum(score_form + "," + query_form + "->" + key_form, dscore, queries.astype(jnp.float32)) * scaling
    return query_part_grad, key_part_grad, value_part_grad


def combine_stats(max_band, sum_band, dot_band, max_strided, sum_strided, dot_strided):
    top = jnp.maximum(max_band, max_strided)
    band_factor = jnp.exp(max_band - top)
    strided_factor = jnp.exp(max_strided - top)
    total = band_factor * sum_band + strided_factor * sum_strided
    delta = (band_factor * dot_band + strided_factor * dot_strided) / total
    return band_factor, strided_factor, total, top + jnp.log(total), delta


def band_view(values):
    return values.reshape(TOKENS // BLOCK, BLOCK, values.shape[-1])


def band_back(values):
    return values.reshape((TOKENS,) + values.shape[2:])


def strided_view(values):
    return jnp.swapaxes(values.reshape((N_SEQ, STRIDE) + values.shape[1:]), 0, 1)


def strided_back(values):
    return jnp.swapaxes(values, 0, 1).reshape((TOKENS,) + values.shape[2:])


def reference(query_rows, key_rows, value_rows, out_grad, out_weight):
    grad_attended = jnp.dot(out_grad, out_weight.T, preferred_element_type=jnp.float32).astype(jnp.bfloat16)
    band_rows = lax.broadcasted_iota(jnp.int32, (BLOCK, BLOCK), 0)
    band_cols = lax.broadcasted_iota(jnp.int32, (BLOCK, BLOCK), 1)
    band_visible = band_cols <= band_rows
    far_rows = lax.broadcasted_iota(jnp.int32, (N_SEQ, N_SEQ), 0)
    far_cols = lax.broadcasted_iota(jnp.int32, (N_SEQ, N_SEQ), 1)
    strided_visible = far_cols < far_rows
    band_forms = ("bid", "bjd", "bij")
    strided_forms = ("sid", "sjd", "sij")

    def one_head(head_index):
        start = (head_index * DH).astype(jnp.int32)
        query_head = lax.dynamic_slice_in_dim(query_rows, start, DH, 1)
        key_head = lax.dynamic_slice_in_dim(key_rows, start, DH, 1)
        value_head = lax.dynamic_slice_in_dim(value_rows, start, DH, 1)
        grad_head = lax.dynamic_slice_in_dim(grad_attended, start, DH, 1)
        band_scores, max_band, sum_band, out_band = part_forward(band_view(query_head), band_view(key_head), band_view(value_head), band_visible, band_forms)
        strided_scores, max_strided, sum_strided, out_strided = part_forward(strided_view(query_head), strided_view(key_head), strided_view(value_head), strided_visible, strided_forms)
        max_band, sum_band, out_band = band_back(max_band), band_back(sum_band), band_back(out_band)
        max_strided, sum_strided, out_strided = strided_back(max_strided), strided_back(sum_strided), strided_back(out_strided)
        grad_float = grad_head.astype(jnp.float32)
        dot_band = jnp.sum(grad_float * out_band, axis=-1)
        dot_strided = jnp.sum(grad_float * out_strided, axis=-1)
        band_factor, strided_factor, total, lse, delta = combine_stats(max_band, sum_band, dot_band, max_strided, sum_strided, dot_strided)
        attended_head = ((band_factor[:, None] * out_band + strided_factor[:, None] * out_strided) / total[:, None]).astype(jnp.bfloat16)
        band_grads = part_backward(band_scores, band_visible, band_view(lse[:, None])[..., 0], band_view(delta[:, None])[..., 0], band_view(query_head), band_view(key_head), band_view(value_head), band_view(grad_head), band_forms)
        strided_grads = part_backward(strided_scores, strided_visible, strided_view(lse), strided_view(delta), strided_view(query_head), strided_view(key_head), strided_view(value_head), strided_view(grad_head), strided_forms)
        results = [attended_head]
        for which in range(3):
            results.append((band_back(band_grads[which]) + rounded(strided_back(strided_grads[which]))).astype(jnp.bfloat16))
        return tuple(results)

    stacked = lax.map(one_head, jnp.arange(HEADS, dtype=jnp.int32))

    def to_rows(values):
        return jnp.swapaxes(values, 0, 1).reshape(TOKENS, HEADS * DH)

    return (to_rows(stacked[0]), to_rows(stacked[1]), to_rows(stacked[2]), to_rows(stacked[3]))
```

```python
import functools

import jax
import jax.numpy as jnp
from jax import lax
from jax.experimental import pallas as pl
from jax.experimental.pallas import tpu as pltpu
from jax.sharding import Mesh
from jax.sharding import PartitionSpec as P

DH = 128
BLOCK = 128
SCALING = DH ** (-0.5)
SENTINEL = -1e30
SEQ = ("x", "zl", "y", "core")
UNITS = 16
F32 = jnp.float32
BF16 = jnp.bfloat16


def nt(a, b):
    return lax.dot_general(a, b, (((1,), (1,)), ((), ())), preferred_element_type=F32)


def tn(a, b):
    return lax.dot_general(a, b, (((0,), (0,)), ((), ())), preferred_element_type=F32)


def nn(a, b):
    return lax.dot_general(a, b, (((1,), (0,)), ((), ())), preferred_element_type=F32)


def swap_matrix():
    rows = lax.broadcasted_iota(jnp.int32, (256, 256), 0)
    cols = lax.broadcasted_iota(jnp.int32, (256, 256), 1)
    return jnp.where(cols == (rows % 16) * 16 + rows // 16, 1.0, 0.0).astype(BF16)


def spread_matrix():
    rows = lax.broadcasted_iota(jnp.int32, (128, 16), 0)
    cols = lax.broadcasted_iota(jnp.int32, (128, 16), 1)
    return jnp.where(rows == cols * 8, 1.0, 0.0).astype(BF16)


def collect_matrix():
    rows = lax.broadcasted_iota(jnp.int32, (16, 128), 0)
    cols = lax.broadcasted_iota(jnp.int32, (16, 128), 1)
    return jnp.where(cols == rows * 8, 1.0, 0.0).astype(BF16)


def split_rows(rows):
    hi = rows.astype(BF16).astype(F32)
    mid = (rows - hi).astype(BF16).astype(F32)
    low = (rows - hi - mid).astype(BF16).astype(F32)
    return jnp.concatenate([hi, mid, low, jnp.zeros_like(hi)], axis=0)


def join_rows(parts):
    return parts[0:32] + parts[32:64] + parts[64:96]


def send_stats(stats, out_ref, base):
    columns = jnp.transpose(split_rows(stats))
    spread = spread_matrix()
    for block in range(8):
        piece = columns[block * 16 : block * 16 + 16].astype(BF16)
        rows = nn(spread, piece).astype(BF16).reshape(16, 8, 128)
        out_ref[block * 16 : block * 16 + 16, base : base + 8, :] = rows


def take_stats(in_ref, base):
    collect = collect_matrix()
    pieces = []
    for block in range(8):
        rows = in_ref[block * 16 : block * 16 + 16, base : base + 8, :].reshape(128, 128)
        pieces.append(nn(collect, rows))
    return join_rows(jnp.transpose(jnp.concatenate(pieces, axis=0)))


def pack_rows(sources, out_ref):
    swap = swap_matrix()

    def step(block, carry):
        at = pl.multiple_of(block * 16, 16)
        for which, source in enumerate(sources):
            pieces = []
            for unit in range(UNITS):
                row, head = unit // 4, unit % 4
                pieces.append(
                    source[pl.ds(row * 128 + at, 16), head * 128 : head * 128 + 128]
                )
            moved = nn(swap, jnp.concatenate(pieces, axis=0)).astype(BF16)
            out_ref[pl.ds(at, 16), which * 16 : which * 16 + 16, :] = moved.reshape(
                16, 16, 128
            )
        return carry

    lax.fori_loop(0, 8, step, 0)


def pack_kernel(q_ref, k_ref, v_ref, out_ref):
    pack_rows((q_ref, k_ref, v_ref), out_ref)


def masks(strict):
    keys = lax.broadcasted_iota(jnp.int32, (128, 128), 0)
    queries = lax.broadcasted_iota(jnp.int32, (128, 128), 1)
    return keys < queries if strict else keys <= queries


def forward_rows(q, k, visible):
    scores = nt(k, q) * SCALING
    top = jnp.max(jnp.where(visible, scores, SENTINEL), axis=0, keepdims=True)
    weights = jnp.where(visible, jnp.exp(scores - top), 0.0)
    total = jnp.sum(weights, axis=0, keepdims=True)
    return scores, top, weights, total


def band_kernel(q_ref, k_ref, v_ref, g_ref, out_ref, stats_ref):
    pack_rows((g_ref,), out_ref)
    visible = masks(False)

    for unit in range(UNITS):
        rows = slice((unit // 4) * 128, (unit // 4) * 128 + 128)
        cols = slice((unit % 4) * 128, (unit % 4) * 128 + 128)
        q, k, v, g = q_ref[rows, cols], k_ref[rows, cols], v_ref[rows, cols], g_ref[rows, cols]
        _, top, weights, total = forward_rows(q, k, visible)
        dot = jnp.sum(weights * nt(v, g), axis=0, keepdims=True)
        stats_ref[unit : unit + 1, :] = top + jnp.log(total)
        stats_ref[16 + unit : 17 + unit, :] = dot / total
    send_stats(stats_ref[...], out_ref, 16)


def far_kernel(qkv_ref, g_ref, out_ref, in_scr, out_scr, stats_ref):
    swap = swap_matrix()
    visible = masks(True)

    def unpack(block, carry):
        at = pl.multiple_of(block * 16, 16)
        for which in range(4):
            source = g_ref if which == 3 else qkv_ref
            base = 0 if which == 3 else which * 16
            rows = source[pl.ds(at, 16), base : base + 16, :].reshape(256, 128)
            in_scr[which, :, pl.ds(at, 16), :] = (
                nn(swap, rows).astype(BF16).reshape(16, 16, 128)
            )
        return carry

    lax.fori_loop(0, 8, unpack, 0)
    band = take_stats(g_ref, 16)
    for unit in range(UNITS):
        q, k, v, g = in_scr[0, unit], in_scr[1, unit], in_scr[2, unit], in_scr[3, unit]
        band_lse = band[unit : unit + 1]
        band_delta = band[16 + unit : 17 + unit]
        _, top, weights, total = forward_rows(q, k, visible)
        highest = jnp.maximum(band_lse, top)
        band_part = jnp.exp(band_lse - highest)
        far_part = jnp.exp(top - highest)
        norm = band_part + far_part * total
        lse = highest + jnp.log(norm)
        probs = weights * (far_part / norm)
        rounded = probs.astype(BF16)
        dprob = nt(v, g)
        delta = band_delta * (band_part / norm) + jnp.sum(probs * dprob, axis=0, keepdims=True)
        dscore = (probs * (dprob - delta)).astype(BF16)
        out_scr[0, unit] = tn(rounded, v).astype(BF16)
        out_scr[1, unit] = (tn(dscore, k) * SCALING).astype(BF16)
        out_scr[2, unit] = (nn(dscore, q) * SCALING).astype(BF16)
        out_scr[3, unit] = nn(rounded, g).astype(BF16)
        stats_ref[unit : unit + 1, :] = lse
        stats_ref[16 + unit : 17 + unit, :] = delta

    def pack(block, carry):
        at = pl.multiple_of(block * 16, 16)
        for which in range(4):
            rows = out_scr[which, :, pl.ds(at, 16), :].reshape(256, 128)
            out_ref[pl.ds(at, 16), which * 16 : which * 16 + 16, :] = (
                nn(swap, rows).astype(BF16).reshape(16, 16, 128)
            )
        return carry

    lax.fori_loop(0, 8, pack, 0)
    send_stats(stats_ref[...], out_ref, 64)


def final_kernel(q_ref, k_ref, v_ref, g_ref, far_ref, att_ref, dq_ref, dk_ref, dv_ref, far_scr):
    swap = swap_matrix()
    visible = masks(False)

    def unpack(block, carry):
        at = pl.multiple_of(block * 16, 16)
        for which in range(4):
            rows = far_ref[pl.ds(at, 16), which * 16 : which * 16 + 16, :].reshape(256, 128)
            far_scr[which, :, pl.ds(at, 16), :] = (
                nn(swap, rows).astype(BF16).reshape(16, 16, 128)
            )
        return carry

    lax.fori_loop(0, 8, unpack, 0)
    stats = take_stats(far_ref, 64)
    for unit in range(UNITS):
        rows = slice((unit // 4) * 128, (unit // 4) * 128 + 128)
        cols = slice((unit % 4) * 128, (unit % 4) * 128 + 128)
        q, k, v, g = q_ref[rows, cols], k_ref[rows, cols], v_ref[rows, cols], g_ref[rows, cols]
        lse = stats[unit : unit + 1]
        delta = stats[16 + unit : 17 + unit]
        scores = nt(k, q) * SCALING
        probs = jnp.where(visible, jnp.exp(scores - lse), 0.0)
        rounded = probs.astype(BF16)
        dscore = (probs * (nt(v, g) - delta)).astype(BF16)
        far = [far_scr[which, unit].astype(F32) for which in range(4)]
        att_ref[rows, cols] = (tn(rounded, v) + far[0]).astype(BF16)
        dq_ref[rows, cols] = (tn(dscore, k) * SCALING + far[1]).astype(BF16)
        dk_ref[rows, cols] = (nn(dscore, q) * SCALING + far[2]).astype(BF16)
        dv_ref[rows, cols] = (nn(rounded, g) + far[3]).astype(BF16)


def call(kernel, args, outs, scratch=()):
    vmem = pl.BlockSpec(memory_space=pltpu.VMEM)
    single = not isinstance(outs, tuple)
    return pl.pallas_call(
        kernel,
        out_shape=outs,
        in_specs=[vmem] * len(args),
        out_specs=vmem if single else tuple([vmem] * len(outs)),
        scratch_shapes=list(scratch),
        compiler_params=pltpu.CompilerParams(vmem_limit_bytes=56 * 1024 * 1024),
    )(*args)


def shifted(values, axis, by):
    return lax.ppermute(values, axis, [(i, (i + by) % 4) for i in range(4)])


def around(values, axis):
    return jnp.concatenate(
        [values] + [shifted(values, axis, by) for by in (1, 2, 3)], axis=0
    )


def column_order(width):
    zl, y, core = lax.axis_index("zl"), lax.axis_index("y"), lax.axis_index("core")
    rows = lax.broadcasted_iota(jnp.int32, (width, width), 0)
    cols = lax.broadcasted_iota(jnp.int32, (width, width), 1)
    core_at = (cols // 512 + core) % 2
    y_at = (y - (cols // 128) % 4 + 4) % 4
    zl_at = (zl - (cols // 32) % 4 + 4) % 4
    source = zl_at * 256 + y_at * 64 + core_at * 32 + cols % 32
    return (rows == source).astype(BF16)


def local(query_rows, key_rows, value_rows, out_grad, out_weight):
    tokens, width = query_rows.shape
    x, head = lax.axis_index("x"), lax.axis_index("head")

    sent = call(
        pack_kernel,
        (query_rows, key_rows, value_rows),
        jax.ShapeDtypeStruct((128, 48, 128), BF16),
    )
    weight = lax.ppermute(
        out_weight.T,
        ("x", "head"),
        [(a * 4 + h, h * 4 + a) for a in range(4) for h in range(4)],
    )
    weight = around(around(weight, "zl"), "y")
    half = weight.shape[0] // 2
    before, after = shifted(weight, "x", 1), shifted(weight, "x", -1)
    across = jnp.concatenate(
        [shifted(before[:half], "x", 1), shifted(after[half:], "x", -1)], axis=0
    )
    pieces = [weight, before, across, after]
    others = [lax.ppermute(piece, "core", [(0, 1), (1, 0)]) for piece in pieces]

    ordered = jnp.dot(out_grad, column_order(out_grad.shape[1]), preferred_element_type=F32)
    ordered = ordered.astype(BF16)
    partials = jnp.stack(
        [
            jnp.dot(ordered[:, :512], own, preferred_element_type=F32)
            + jnp.dot(ordered[:, 512:], other, preferred_element_type=F32)
            for own, other in zip(pieces, others)
        ]
    )
    far_qkv = lax.all_to_all(sent, SEQ, 0, 0, tiled=True)
    far_qkv, partials = lax.optimization_barrier((far_qkv, partials))
    middle = tokens // 2

    def partial(target, low):
        chosen = lax.dynamic_index_in_dim(partials, (x - target + 8) % 4, 0, keepdims=False)
        return chosen[:middle] if low else chosen[middle:]

    up = partial(head - 1, True).astype(BF16)
    down = partial(head + 1, False).astype(BF16)
    for step in (1, 2, 3):
        from_below = shifted(up, "head", 1)
        from_above = shifted(down, "head", -1)
        up = (from_below.astype(F32) + partial(head - 1 - step, True)).astype(BF16)
        down = (from_above.astype(F32) + partial(head + 1 + step, False)).astype(BF16)
    grad_rows = jnp.concatenate([up, down], axis=0)

    sent_grad = call(
        band_kernel,
        (query_rows, key_rows, value_rows, grad_rows),
        jax.ShapeDtypeStruct((128, 24, 128), BF16),
        (pltpu.VMEM((32, 128), F32),),
    )
    far_grad = lax.all_to_all(sent_grad, SEQ, 0, 0, tiled=True)
    back = call(
        far_kernel,
        (far_qkv, far_grad),
        jax.ShapeDtypeStruct((128, 72, 128), BF16),
        (
            pltpu.VMEM((4, 16, 128, 128), BF16),
            pltpu.VMEM((4, 16, 128, 128), BF16),
            pltpu.VMEM((32, 128), F32),
        ),
    )
    home = lax.all_to_all(back, SEQ, 0, 0, tiled=True)
    shape = jax.ShapeDtypeStruct((tokens, width), BF16)
    return call(
        final_kernel,
        (query_rows, key_rows, value_rows, grad_rows, home),
        (shape, shape, shape, shape),
        (pltpu.VMEM((4, 16, 128, 128), BF16),),
    )


def solution(mesh):
    fine = Mesh(mesh.devices.reshape(4, 4, 4, 2, 4), ("x", "zl", "y", "core", "head"))
    rows = P(SEQ, "head")
    return jax.shard_map(
        local,
        mesh=fine,
        in_specs=(rows, rows, rows, rows, P("head", SEQ)),
        out_specs=(rows, rows, rows, rows),
        check_vma=False,
    )
```

```python
import jax
import jax.numpy as jnp
from jax import lax
from jax.experimental import pallas as pl
from jax.experimental.pallas import tpu as pltpu
from jax.sharding import Mesh
from jax.sharding import PartitionSpec as P

DH = 128
SCALING = DH ** (-0.5)
SENTINEL = -1e30
SEQ = ("x", "zl", "y", "core")
UNITS = 16
F32 = jnp.float32
BF16 = jnp.bfloat16


def nt(a, b):
    return lax.dot_general(a, b, (((1,), (1,)), ((), ())), preferred_element_type=F32)


def tn(a, b):
    return lax.dot_general(a, b, (((0,), (0,)), ((), ())), preferred_element_type=F32)


def nn(a, b):
    return lax.dot_general(a, b, (((1,), (0,)), ((), ())), preferred_element_type=F32)


def swap_matrix():
    rows = lax.broadcasted_iota(jnp.int32, (256, 256), 0)
    cols = lax.broadcasted_iota(jnp.int32, (256, 256), 1)
    return jnp.where(cols == (rows % 16) * 16 + rows // 16, 1.0, 0.0).astype(BF16)


def one_hot_rows(rows_n, cols_n, row, spread):
    rows = lax.broadcasted_iota(jnp.int32, (rows_n, cols_n), 0)
    cols = lax.broadcasted_iota(jnp.int32, (rows_n, cols_n), 1)
    hit = rows == cols * 8 + row if spread else cols == rows * 8 + row
    return jnp.where(hit, 1.0, 0.0).astype(BF16)


def split_rows(rows):
    hi = rows.astype(BF16).astype(F32)
    mid = (rows - hi).astype(BF16).astype(F32)
    low = (rows - hi - mid).astype(BF16).astype(F32)
    return jnp.concatenate([hi, mid, low, jnp.zeros_like(hi)], axis=0)


def join_rows(parts):
    return parts[0:32] + parts[32:64] + parts[64:96]


def stat_columns(stats):
    return jnp.transpose(split_rows(stats)).astype(BF16)


def take_stats(in_ref, base, row):
    collect = one_hot_rows(16, 128, row, False)
    pieces = []
    for block in range(8):
        rows = in_ref[block * 16 : block * 16 + 16, base : base + 8, :].reshape(128, 128)
        pieces.append(nn(collect, rows))
    return join_rows(jnp.transpose(jnp.concatenate(pieces, axis=0)))


def pack_rows(sources, out_ref):
    swap = swap_matrix()

    def step(block, carry):
        at = pl.multiple_of(block * 16, 16)
        for which, source in enumerate(sources):
            pieces = []
            for unit in range(UNITS):
                row, head = unit // 4, unit % 4
                pieces.append(
                    source[pl.ds(row * 128 + at, 16), head * 128 : head * 128 + 128]
                )
            moved = nn(swap, jnp.concatenate(pieces, axis=0)).astype(BF16)
            out_ref[pl.ds(at, 16), which * 16 : which * 16 + 16, :] = moved.reshape(
                16, 16, 128
            )
        return carry

    lax.fori_loop(0, 8, step, 0)


def pack_kernel(q_ref, k_ref, v_ref, out_ref):
    pack_rows((q_ref, k_ref, v_ref), out_ref)


def masks(strict):
    keys = lax.broadcasted_iota(jnp.int32, (128, 128), 0)
    queries = lax.broadcasted_iota(jnp.int32, (128, 128), 1)
    return keys < queries if strict else keys <= queries


def forward_rows(q, k, visible):
    scores = nt(k, q) * SCALING
    top = jnp.max(jnp.where(visible, scores, SENTINEL), axis=0, keepdims=True)
    weights = jnp.where(visible, jnp.exp(scores - top), 0.0)
    total = jnp.sum(weights, axis=0, keepdims=True)
    return scores, top, weights, total


def far_forward_kernel(qkv_ref, unit_ref, out_ref, columns_ref, lse_ref, out_scr):
    swap = swap_matrix()
    visible = masks(True)

    def unpack(block, carry):
        at = pl.multiple_of(block * 16, 16)
        for which in range(3):
            rows = qkv_ref[pl.ds(at, 16), which * 16 : which * 16 + 16, :].reshape(256, 128)
            unit_ref[which, :, pl.ds(at, 16), :] = (
                nn(swap, rows).astype(BF16).reshape(16, 16, 128)
            )
        return carry

    lax.fori_loop(0, 8, unpack, 0)
    lse_ref[...] = jnp.zeros((32, 128), F32)
    for unit in range(UNITS):
        q, k, v = unit_ref[0, unit], unit_ref[1, unit], unit_ref[2, unit]
        _, top, weights, total = forward_rows(q, k, visible)
        some = total > 0.0
        inverse = jnp.where(some, 1.0 / jnp.where(some, total, 1.0), 0.0)
        out_scr[unit] = tn((weights * inverse).astype(BF16), v).astype(BF16)
        lse_ref[unit : unit + 1, :] = jnp.where(
            some, top + jnp.log(jnp.where(some, total, 1.0)), SENTINEL
        )

    def pack(block, carry):
        at = pl.multiple_of(block * 16, 16)
        rows = out_scr[:, pl.ds(at, 16), :].reshape(256, 128)
        out_ref[pl.ds(at, 16), :, :] = nn(swap, rows).astype(BF16).reshape(16, 16, 128)
        return carry

    lax.fori_loop(0, 8, pack, 0)
    columns_ref[...] = stat_columns(lse_ref[...])


def band_kernel(q_ref, k_ref, v_ref, g_ref, far_ref, columns_ref, out_ref, stats_ref):
    pack_rows((g_ref,), out_ref)
    out_ref[:, 16:32, :] = far_ref[...]
    visible = masks(False)

    for unit in range(UNITS):
        rows = slice((unit // 4) * 128, (unit // 4) * 128 + 128)
        cols = slice((unit % 4) * 128, (unit % 4) * 128 + 128)
        q, k, v, g = q_ref[rows, cols], k_ref[rows, cols], v_ref[rows, cols], g_ref[rows, cols]
        _, top, weights, total = forward_rows(q, k, visible)
        dot = jnp.sum(weights * nt(v, g), axis=0, keepdims=True)
        stats_ref[unit : unit + 1, :] = top + jnp.log(total)
        stats_ref[16 + unit : 17 + unit, :] = dot / total
    columns = stat_columns(stats_ref[...])
    home, away = one_hot_rows(128, 16, 0, True), one_hot_rows(128, 16, 1, True)
    for block in range(8):
        at = slice(block * 16, block * 16 + 16)
        rows = nn(home, columns[at]) + nn(away, columns_ref[at, :])
        out_ref[at, 32:40, :] = rows.astype(BF16).reshape(16, 8, 128)


def combine(band_lse, far_lse):
    highest = jnp.maximum(band_lse, far_lse)
    band_part = jnp.exp(band_lse - highest)
    far_part = jnp.exp(far_lse - highest)
    norm = band_part + far_part
    return highest + jnp.log(norm), band_part / norm, far_part / norm


def far_backward_kernel(unit_ref, lse_ref, g_ref, out_ref, g_scr, out_scr):
    swap = swap_matrix()
    visible = masks(True)

    def unpack(block, carry):
        at = pl.multiple_of(block * 16, 16)
        rows = g_ref[pl.ds(at, 16), 0:16, :].reshape(256, 128)
        g_scr[:, pl.ds(at, 16), :] = nn(swap, rows).astype(BF16).reshape(16, 16, 128)
        return carry

    lax.fori_loop(0, 8, unpack, 0)
    band = take_stats(g_ref, 32, 0)
    lse, band_share, _ = combine(band[0:16], lse_ref[0:16, :])
    band_delta = band_share * band[16:32]
    for unit in range(UNITS):
        q, k, v, g = unit_ref[0, unit], unit_ref[1, unit], unit_ref[2, unit], g_scr[unit]
        scores = nt(k, q) * SCALING
        probs = jnp.where(visible, jnp.exp(scores - lse[unit : unit + 1]), 0.0)
        dprob = nt(v, g)
        delta = band_delta[unit : unit + 1] + jnp.sum(probs * dprob, axis=0, keepdims=True)
        dscore = (probs * (dprob - delta)).astype(BF16)
        out_scr[0, unit] = (tn(dscore, k) * SCALING).astype(BF16)
        out_scr[1, unit] = (nn(dscore, q) * SCALING).astype(BF16)
        out_scr[2, unit] = nn(probs.astype(BF16), g).astype(BF16)

    def pack(block, carry):
        at = pl.multiple_of(block * 16, 16)
        for which in range(3):
            rows = out_scr[which, :, pl.ds(at, 16), :].reshape(256, 128)
            out_ref[pl.ds(at, 16), which * 16 : which * 16 + 16, :] = (
                nn(swap, rows).astype(BF16).reshape(16, 16, 128)
            )
        return carry

    lax.fori_loop(0, 8, pack, 0)


def band_backward_kernel(
    q_ref, k_ref, v_ref, g_ref, band_ref, far_ref, att_ref, dq_ref, dk_ref, dv_ref, far_scr
):
    swap = swap_matrix()
    visible = masks(False)

    def unpack(block, carry):
        at = pl.multiple_of(block * 16, 16)
        rows = far_ref[pl.ds(at, 16), 16:32, :].reshape(256, 128)
        far_scr[:, pl.ds(at, 16), :] = nn(swap, rows).astype(BF16).reshape(16, 16, 128)
        return carry

    lax.fori_loop(0, 8, unpack, 0)
    far_lse = take_stats(far_ref, 32, 1)[0:16]
    lse, band_share, far_share = combine(band_ref[0:16, :], far_lse)
    band_delta = band_share * band_ref[16:32, :]
    shares = jnp.transpose(
        jnp.concatenate([far_share, jnp.zeros((112, 128), F32)], axis=0)
    )
    ones = jnp.ones((8, 128), BF16)
    for unit in range(UNITS):
        rows = slice((unit // 4) * 128, (unit // 4) * 128 + 128)
        cols = slice((unit % 4) * 128, (unit % 4) * 128 + 128)
        q, k, v, g = q_ref[rows, cols], k_ref[rows, cols], v_ref[rows, cols], g_ref[rows, cols]
        out_far = far_scr[unit].astype(F32)
        product = g.astype(F32) * out_far
        high = product.astype(BF16)
        low = (product - high.astype(F32)).astype(BF16)
        dot_far = (nt(ones, high) + nt(ones, low))[0:1]
        delta = band_delta[unit : unit + 1] + far_share[unit : unit + 1] * dot_far
        scores = nt(k, q) * SCALING
        probs = jnp.where(visible, jnp.exp(scores - lse[unit : unit + 1]), 0.0)
        rounded = probs.astype(BF16)
        dscore = (probs * (nt(v, g) - delta)).astype(BF16)
        att_ref[rows, cols] = (tn(rounded, v) + shares[:, unit : unit + 1] * out_far).astype(BF16)
        dq_ref[rows, cols] = tn(dscore, k) * SCALING
        dk_ref[rows, cols] = nn(dscore, q) * SCALING
        dv_ref[rows, cols] = nn(rounded, g)


def final_kernel(dq_ref, dk_ref, dv_ref, far_ref, query_ref, key_ref, value_ref):
    bands, outs = (dq_ref, dk_ref, dv_ref), (query_ref, key_ref, value_ref)
    rows = lax.broadcasted_iota(jnp.int32, (64, 256), 0)
    cols = lax.broadcasted_iota(jnp.int32, (64, 256), 1)
    source = (rows % 16) * 16 + pl.program_id(0) * 4 + rows // 16
    choose = jnp.where(cols == source, 1.0, 0.0).astype(BF16)
    for block in range(8):
        place = slice(block * 16, block * 16 + 16)
        for which in range(3):
            far = far_ref[place, which * 16 : which * 16 + 16, :].reshape(256, 128)
            moved = nn(choose, far)
            for head in range(4):
                at = slice(head * 128, head * 128 + 128)
                piece = moved[head * 16 : head * 16 + 16]
                outs[which][place, at] = (bands[which][place, at] + piece).astype(BF16)


def final_call(bands, home, shape):
    rows = pl.BlockSpec((128, shape.shape[1]), lambda step: (step, 0))
    whole = pl.BlockSpec(home.shape, lambda step: (0, 0, 0))
    return pl.pallas_call(
        final_kernel,
        grid=(4,),
        out_shape=(shape,) * 3,
        in_specs=[rows] * 3 + [whole],
        out_specs=(rows,) * 3,
        compiler_params=pltpu.CompilerParams(vmem_limit_bytes=16 * 1024 * 1024),
    )(*[pltpu.with_memory_space_constraint(band, pltpu.HBM) for band in bands], home)


def call(kernel, args, outs, scratch=()):
    vmem = pl.BlockSpec(memory_space=pltpu.VMEM)
    single = not isinstance(outs, tuple)
    return pl.pallas_call(
        kernel,
        out_shape=outs,
        in_specs=[vmem] * len(args),
        out_specs=vmem if single else tuple([vmem] * len(outs)),
        scratch_shapes=list(scratch),
        compiler_params=pltpu.CompilerParams(vmem_limit_bytes=24 * 1024 * 1024),
    )(*args)


def shifted(values, axis, by):
    return lax.ppermute(values, axis, [(i, (i + by) % 4) for i in range(4)])


def gathered(values, axis):
    return [values] + [shifted(values, axis, by) for by in (1, 2, 3)]


def in_order(blocks, mine):
    rising = jnp.concatenate(blocks[::-1] + blocks[::-1], axis=0)
    return lax.dynamic_slice_in_dim(rising, 3 - mine, 4, 0)


def program(query_rows, key_rows, value_rows, out_grad, out_weight):
    tokens, width = query_rows.shape
    x, zl, y, core, head = (lax.axis_index(name) for name in (*SEQ, "head"))
    middle = tokens // 2

    below, above = shifted(out_grad, "head", 1), shifted(out_grad, "head", -1)
    opposite_low = shifted(below[:middle], "head", 1)
    opposite_high = shifted(above[middle:], "head", -1)

    sent = call(
        pack_kernel,
        (query_rows, key_rows, value_rows),
        jax.ShapeDtypeStruct((128, 48, 128), BF16),
    )
    far_qkv = lax.all_to_all(sent, SEQ, 0, 0, tiled=True)
    weight = in_order(gathered(out_weight.T[None], "zl"), zl)
    weight = in_order(gathered(weight[None], "y"), y)
    weight = jnp.stack(gathered(weight, "x"))
    swapped = lax.ppermute(weight, "core", [(0, 1), (1, 0)])
    first, second = jnp.where(core == 0, weight, swapped), jnp.where(core == 0, swapped, weight)
    weights = jnp.stack([first, second], axis=3).transpose(0, 2, 1, 3, 4, 5)
    weights = weights.reshape(4, -1, weight.shape[-1])

    def rows_for(source):
        return lax.dynamic_index_in_dim(weights, (x - source + 8) % 4, 0, keepdims=False)

    def product(columns, chosen):
        return jnp.dot(columns, chosen, preferred_element_type=F32)

    stats = jax.ShapeDtypeStruct((32, 128), F32)
    units = pltpu.VMEM((16, 128, 128), BF16)
    unit_qkv, far_out, far_columns, far_lse = call(
        far_forward_kernel,
        (far_qkv,),
        (
            jax.ShapeDtypeStruct((3, 16, 128, 128), BF16),
            jax.ShapeDtypeStruct((128, 16, 128), BF16),
            jax.ShapeDtypeStruct((128, 128), BF16),
            stats,
        ),
        (units,),
    )
    early = (
        product(out_grad, rows_for(head))
        + product(below, rows_for(head - 1))
        + product(above, rows_for(head + 1))
    )
    chosen, early, far_out = lax.optimization_barrier((rows_for(head + 2), early, far_out))
    late = jnp.concatenate(
        [product(opposite_low, chosen), product(opposite_high, chosen)], axis=0
    )
    grad_rows = (early + late).astype(BF16)
    sent_grad, band_stats = call(
        band_kernel,
        (query_rows, key_rows, value_rows, grad_rows, far_out, far_columns),
        (jax.ShapeDtypeStruct((128, 40, 128), BF16), stats),
    )
    crossed = lax.all_to_all(sent_grad, SEQ, 0, 0, tiled=True)
    returned = call(
        far_backward_kernel,
        (unit_qkv, far_lse, crossed),
        jax.ShapeDtypeStruct((128, 48, 128), BF16),
        (units, pltpu.VMEM((3, 16, 128, 128), BF16)),
    )
    home = lax.all_to_all(returned, SEQ, 0, 0, tiled=True)
    shape = jax.ShapeDtypeStruct((tokens, width), BF16)
    wide = jax.ShapeDtypeStruct((tokens, width), F32)
    attended, dq, dk, dv = call(
        band_backward_kernel,
        (query_rows, key_rows, value_rows, grad_rows, band_stats, crossed),
        (shape, wide, wide, wide),
        (units,),
    )
    grads = final_call((dq, dk, dv), home, shape)
    return (attended, *grads)


def solution(mesh):
    fine = Mesh(mesh.devices.reshape(4, 4, 4, 2, 4), ("x", "zl", "y", "core", "head"))
    rows = P(SEQ, "head")
    return jax.shard_map(
        program,
        mesh=fine,
        in_specs=(rows, rows, rows, rows, P("head", SEQ)),
        out_specs=(rows, rows, rows, rows),
        check_vma=False,
    )
```

```python
import jax
import jax.numpy as jnp
from jax import lax
from jax.experimental import pallas as pl
from jax.experimental.pallas import tpu as pltpu
from jax.sharding import Mesh
from jax.sharding import PartitionSpec as P

DH = 128
SCALING = DH ** (-0.5)
SENTINEL = -1e30
SEQ = ("x", "zl", "y", "core")
UNITS = 16
F32 = jnp.float32
BF16 = jnp.bfloat16


def nt(a, b):
    return lax.dot_general(a, b, (((1,), (1,)), ((), ())), preferred_element_type=F32)


def tn(a, b):
    return lax.dot_general(a, b, (((0,), (0,)), ((), ())), preferred_element_type=F32)


def nn(a, b):
    return lax.dot_general(a, b, (((1,), (0,)), ((), ())), preferred_element_type=F32)


def swap_matrix():
    rows = lax.broadcasted_iota(jnp.int32, (256, 256), 0)
    cols = lax.broadcasted_iota(jnp.int32, (256, 256), 1)
    return jnp.where(cols == (rows % 16) * 16 + rows // 16, 1.0, 0.0).astype(BF16)


def one_hot_rows(rows_n, cols_n, row, spread):
    rows = lax.broadcasted_iota(jnp.int32, (rows_n, cols_n), 0)
    cols = lax.broadcasted_iota(jnp.int32, (rows_n, cols_n), 1)
    hit = rows == cols * 8 + row if spread else cols == rows * 8 + row
    return jnp.where(hit, 1.0, 0.0).astype(BF16)


def split_rows(rows):
    hi = rows.astype(BF16).astype(F32)
    mid = (rows - hi).astype(BF16).astype(F32)
    low = (rows - hi - mid).astype(BF16).astype(F32)
    return jnp.concatenate([hi, mid, low, jnp.zeros_like(hi)], axis=0)


def join_rows(parts):
    return parts[0:32] + parts[32:64] + parts[64:96]


def stat_columns(stats):
    return jnp.transpose(split_rows(stats)).astype(BF16)


def take_stats(in_ref, base, row):
    collect = one_hot_rows(16, 128, row, False)
    pieces = []
    for block in range(8):
        rows = in_ref[block * 16 : block * 16 + 16, base : base + 8, :].reshape(128, 128)
        pieces.append(nn(collect, rows))
    return join_rows(jnp.transpose(jnp.concatenate(pieces, axis=0)))


def pack_rows(sources, out_ref):
    swap = swap_matrix()

    def step(block, carry):
        at = pl.multiple_of(block * 16, 16)
        for which, source in enumerate(sources):
            pieces = []
            for unit in range(UNITS):
                row, head = unit // 4, unit % 4
                pieces.append(
                    source[pl.ds(row * 128 + at, 16), head * 128 : head * 128 + 128]
                )
            moved = nn(swap, jnp.concatenate(pieces, axis=0)).astype(BF16)
            out_ref[pl.ds(at, 16), which * 16 : which * 16 + 16, :] = moved.reshape(
                16, 16, 128
            )
        return carry

    lax.fori_loop(0, 8, step, 0)


def pack_kernel(q_ref, k_ref, v_ref, out_ref):
    pack_rows((q_ref, k_ref, v_ref), out_ref)


def masks(strict):
    keys = lax.broadcasted_iota(jnp.int32, (128, 128), 0)
    queries = lax.broadcasted_iota(jnp.int32, (128, 128), 1)
    return keys < queries if strict else keys <= queries


def forward_rows(q, k, visible):
    scores = nt(k, q) * SCALING
    top = jnp.max(jnp.where(visible, scores, SENTINEL), axis=0, keepdims=True)
    weights = jnp.where(visible, jnp.exp(scores - top), 0.0)
    total = jnp.sum(weights, axis=0, keepdims=True)
    return scores, top, weights, total


def far_forward_kernel(
    qkv_ref, unit_ref, probs_ref, out_ref, columns_ref, lse_ref, out_scr
):
    swap = swap_matrix()
    visible = masks(True)

    def unpack(block, carry):
        at = pl.multiple_of(block * 16, 16)
        for which in range(3):
            rows = qkv_ref[pl.ds(at, 16), which * 16 : which * 16 + 16, :].reshape(256, 128)
            unit_ref[which, :, pl.ds(at, 16), :] = (
                nn(swap, rows).astype(BF16).reshape(16, 16, 128)
            )
        return carry

    lax.fori_loop(0, 8, unpack, 0)
    lse_ref[...] = jnp.zeros((32, 128), F32)
    for unit in range(UNITS):
        q, k, v = unit_ref[0, unit], unit_ref[1, unit], unit_ref[2, unit]
        _, top, weights, total = forward_rows(q, k, visible)
        some = total > 0.0
        inverse = jnp.where(some, 1.0 / jnp.where(some, total, 1.0), 0.0)
        probs = weights * inverse
        probs_ref[unit] = probs
        out_scr[unit] = tn(probs.astype(BF16), v).astype(BF16)
        lse_ref[unit : unit + 1, :] = jnp.where(
            some, top + jnp.log(jnp.where(some, total, 1.0)), SENTINEL
        )

    def pack(block, carry):
        at = pl.multiple_of(block * 16, 16)
        rows = out_scr[:, pl.ds(at, 16), :].reshape(256, 128)
        out_ref[pl.ds(at, 16), :, :] = nn(swap, rows).astype(BF16).reshape(16, 16, 128)
        return carry

    lax.fori_loop(0, 8, pack, 0)
    columns_ref[...] = stat_columns(lse_ref[...])


def band_kernel(q_ref, k_ref, v_ref, g_ref, far_ref, columns_ref, out_ref, stats_ref):
    pack_rows((g_ref,), out_ref)
    out_ref[:, 16:32, :] = far_ref[...]
    visible = masks(False)

    for unit in range(UNITS):
        rows = slice((unit // 4) * 128, (unit // 4) * 128 + 128)
        cols = slice((unit % 4) * 128, (unit % 4) * 128 + 128)
        q, k, v, g = q_ref[rows, cols], k_ref[rows, cols], v_ref[rows, cols], g_ref[rows, cols]
        _, top, weights, total = forward_rows(q, k, visible)
        dot = jnp.sum(weights * nt(v, g), axis=0, keepdims=True)
        stats_ref[unit : unit + 1, :] = top + jnp.log(total)
        stats_ref[16 + unit : 17 + unit, :] = dot / total
    columns = stat_columns(stats_ref[...])
    home, away = one_hot_rows(128, 16, 0, True), one_hot_rows(128, 16, 1, True)
    for block in range(8):
        at = slice(block * 16, block * 16 + 16)
        rows = nn(home, columns[at]) + nn(away, columns_ref[at, :])
        out_ref[at, 32:40, :] = rows.astype(BF16).reshape(16, 8, 128)


def combine(band_lse, far_lse):
    highest = jnp.maximum(band_lse, far_lse)
    band_part = jnp.exp(band_lse - highest)
    far_part = jnp.exp(far_lse - highest)
    norm = band_part + far_part
    return highest + jnp.log(norm), band_part / norm, far_part / norm


def far_backward_kernel(unit_ref, probs_ref, lse_ref, g_ref, out_ref, g_scr, out_scr):
    swap = swap_matrix()

    def unpack(block, carry):
        at = pl.multiple_of(block * 16, 16)
        rows = g_ref[pl.ds(at, 16), 0:16, :].reshape(256, 128)
        g_scr[:, pl.ds(at, 16), :] = nn(swap, rows).astype(BF16).reshape(16, 16, 128)
        return carry

    lax.fori_loop(0, 8, unpack, 0)
    band = take_stats(g_ref, 32, 0)
    _, band_share, far_share = combine(band[0:16], lse_ref[0:16, :])
    band_delta = band_share * band[16:32]
    for unit in range(UNITS):
        q, k, v, g = unit_ref[0, unit], unit_ref[1, unit], unit_ref[2, unit], g_scr[unit]
        probs = probs_ref[unit] * far_share[unit : unit + 1]
        dprob = nt(v, g)
        delta = band_delta[unit : unit + 1] + jnp.sum(probs * dprob, axis=0, keepdims=True)
        dscore = (probs * (dprob - delta)).astype(BF16)
        out_scr[0, unit] = (tn(dscore, k) * SCALING).astype(BF16)
        out_scr[1, unit] = (nn(dscore, q) * SCALING).astype(BF16)
        out_scr[2, unit] = nn(probs.astype(BF16), g).astype(BF16)

    def pack(block, carry):
        at = pl.multiple_of(block * 16, 16)
        for which in range(3):
            rows = out_scr[which, :, pl.ds(at, 16), :].reshape(256, 128)
            out_ref[pl.ds(at, 16), which * 16 : which * 16 + 16, :] = (
                nn(swap, rows).astype(BF16).reshape(16, 16, 128)
            )
        return carry

    lax.fori_loop(0, 8, pack, 0)


def band_backward_kernel(
    q_ref, k_ref, v_ref, g_ref, band_ref, far_ref, att_ref, dq_ref, dk_ref, dv_ref, far_scr
):
    swap = swap_matrix()
    visible = masks(False)

    def unpack(block, carry):
        at = pl.multiple_of(block * 16, 16)
        rows = far_ref[pl.ds(at, 16), 16:32, :].reshape(256, 128)
        far_scr[:, pl.ds(at, 16), :] = nn(swap, rows).astype(BF16).reshape(16, 16, 128)
        return carry

    lax.fori_loop(0, 8, unpack, 0)
    far_lse = take_stats(far_ref, 32, 1)[0:16]
    lse, band_share, far_share = combine(band_ref[0:16, :], far_lse)
    band_delta = band_share * band_ref[16:32, :]
    shares = jnp.transpose(
        jnp.concatenate([far_share, jnp.zeros((112, 128), F32)], axis=0)
    )
    ones = jnp.ones((8, 128), BF16)
    for unit in range(UNITS):
        rows = slice((unit // 4) * 128, (unit // 4) * 128 + 128)
        cols = slice((unit % 4) * 128, (unit % 4) * 128 + 128)
        q, k, v, g = q_ref[rows, cols], k_ref[rows, cols], v_ref[rows, cols], g_ref[rows, cols]
        out_far = far_scr[unit].astype(F32)
        product = g.astype(F32) * out_far
        high = product.astype(BF16)
        low = (product - high.astype(F32)).astype(BF16)
        dot_far = (nt(ones, high) + nt(ones, low))[0:1]
        delta = band_delta[unit : unit + 1] + far_share[unit : unit + 1] * dot_far
        scores = nt(k, q) * SCALING
        probs = jnp.where(visible, jnp.exp(scores - lse[unit : unit + 1]), 0.0)
        rounded = probs.astype(BF16)
        dscore = (probs * (nt(v, g) - delta)).astype(BF16)
        att_ref[rows, cols] = (tn(rounded, v) + shares[:, unit : unit + 1] * out_far).astype(BF16)
        dq_ref[rows, cols] = tn(dscore, k) * SCALING
        dk_ref[rows, cols] = nn(dscore, q) * SCALING
        dv_ref[rows, cols] = nn(rounded, g)


def final_kernel(dq_ref, dk_ref, dv_ref, far_ref, query_ref, key_ref, value_ref):
    bands, outs = (dq_ref, dk_ref, dv_ref), (query_ref, key_ref, value_ref)
    rows = lax.broadcasted_iota(jnp.int32, (64, 256), 0)
    cols = lax.broadcasted_iota(jnp.int32, (64, 256), 1)
    source = (rows % 16) * 16 + pl.program_id(0) * 4 + rows // 16
    choose = jnp.where(cols == source, 1.0, 0.0).astype(BF16)
    for block in range(8):
        place = slice(block * 16, block * 16 + 16)
        for which in range(3):
            far = far_ref[place, which * 16 : which * 16 + 16, :].reshape(256, 128)
            moved = nn(choose, far)
            for head in range(4):
                at = slice(head * 128, head * 128 + 128)
                piece = moved[head * 16 : head * 16 + 16]
                outs[which][place, at] = (bands[which][place, at] + piece).astype(BF16)


def final_call(bands, home, shape):
    rows = pl.BlockSpec((128, shape.shape[1]), lambda step: (step, 0))
    whole = pl.BlockSpec(home.shape, lambda step: (0, 0, 0))
    return pl.pallas_call(
        final_kernel,
        grid=(4,),
        out_shape=(shape,) * 3,
        in_specs=[rows] * 3 + [whole],
        out_specs=(rows,) * 3,
        compiler_params=pltpu.CompilerParams(vmem_limit_bytes=16 * 1024 * 1024),
    )(*[pltpu.with_memory_space_constraint(band, pltpu.HBM) for band in bands], home)


def call(kernel, args, outs, scratch=()):
    vmem = pl.BlockSpec(memory_space=pltpu.VMEM)
    single = not isinstance(outs, tuple)
    return pl.pallas_call(
        kernel,
        out_shape=outs,
        in_specs=[vmem] * len(args),
        out_specs=vmem if single else tuple([vmem] * len(outs)),
        scratch_shapes=list(scratch),
        compiler_params=pltpu.CompilerParams(vmem_limit_bytes=24 * 1024 * 1024),
    )(*args)


def shifted(values, axis, by):
    return lax.ppermute(values, axis, [(i, (i + by) % 4) for i in range(4)])


def around(values, axis):
    return jnp.concatenate(
        [values] + [shifted(values, axis, by) for by in (1, 2, 3)], axis=0
    )


def column_order(width):
    zl, y, core = lax.axis_index("zl"), lax.axis_index("y"), lax.axis_index("core")
    rows = lax.broadcasted_iota(jnp.int32, (width, width), 0)
    cols = lax.broadcasted_iota(jnp.int32, (width, width), 1)
    core_at = (cols // 512 + core) % 2
    y_at = (y - (cols // 128) % 4 + 4) % 4
    zl_at = (zl - (cols // 32) % 4 + 4) % 4
    source = zl_at * 256 + y_at * 64 + core_at * 32 + cols % 32
    return (rows == source).astype(BF16)


def program(query_rows, key_rows, value_rows, out_grad, out_weight):
    tokens, width = query_rows.shape
    x, head = lax.axis_index("x"), lax.axis_index("head")

    sent = call(
        pack_kernel,
        (query_rows, key_rows, value_rows),
        jax.ShapeDtypeStruct((128, 48, 128), BF16),
    )
    own = out_weight.T
    weight = lax.ppermute(
        own,
        ("x", "head"),
        [(a * 4 + h, h * 4 + a) for a in range(4) for h in range(4)],
    )
    weight = around(around(weight, "zl"), "y")
    sent, weight = lax.optimization_barrier((sent, weight))
    far_qkv = lax.all_to_all(sent, SEQ, 0, 0, tiled=True)
    mine = jnp.stack([weight] + [shifted(weight, "x", by) for by in (1, 2, 3)])
    others = lax.ppermute(mine, "core", [(0, 1), (1, 0)])
    ordered = jnp.dot(out_grad, column_order(out_grad.shape[1]), preferred_element_type=F32)
    ordered = ordered.astype(BF16)
    far_qkv, others = lax.optimization_barrier((far_qkv, others))

    def partial(target, mine, others):
        at = (x - target + 8) % 4
        near = lax.dynamic_index_in_dim(mine, at, 0, keepdims=False)
        other = lax.dynamic_index_in_dim(others, at, 0, keepdims=False)
        return jnp.dot(ordered[:, :512], near, preferred_element_type=F32) + jnp.dot(
            ordered[:, 512:], other, preferred_element_type=F32
        )

    middle = tokens // 2
    low, high = slice(0, middle), slice(middle, tokens)

    opposite = partial(head + 2, mine, others).astype(BF16)
    opposite, mine, others = lax.optimization_barrier((opposite, mine, others))
    above, below, here = (partial(head + by, mine, others) for by in (1, -1, 0))
    far_up = shifted(opposite[low], "head", 1)
    far_down = shifted(opposite[high], "head", -1)
    near_up = shifted(above[high].astype(BF16), "head", 1)
    near_down = shifted(below[low].astype(BF16), "head", -1)
    last_up = shifted((far_up.astype(F32) + above[low]).astype(BF16), "head", 1)
    last_down = shifted(
        (far_down.astype(F32) + below[high]).astype(BF16), "head", -1
    )

    stats = jax.ShapeDtypeStruct((32, 128), F32)
    units = pltpu.VMEM((16, 128, 128), BF16)
    unit_qkv, far_probs, far_out, far_columns, far_lse = call(
        far_forward_kernel,
        (far_qkv,),
        (
            jax.ShapeDtypeStruct((3, 16, 128, 128), BF16),
            jax.ShapeDtypeStruct((16, 128, 128), F32),
            jax.ShapeDtypeStruct((128, 16, 128), BF16),
            jax.ShapeDtypeStruct((128, 128), BF16),
            stats,
        ),
        (units,),
    )
    last_up, last_down, far_out = lax.optimization_barrier(
        (last_up, last_down, far_out)
    )
    grad_rows = jnp.concatenate(
        [
            (
                here[low] + near_down.astype(F32) + last_up.astype(F32)
            ).astype(BF16),
            (
                here[high] + near_up.astype(F32) + last_down.astype(F32)
            ).astype(BF16),
        ],
        axis=0,
    )

    sent_grad, band_stats = call(
        band_kernel,
        (query_rows, key_rows, value_rows, grad_rows, far_out, far_columns),
        (jax.ShapeDtypeStruct((128, 40, 128), BF16), stats),
    )
    crossed = lax.all_to_all(sent_grad, SEQ, 0, 0, tiled=True)
    back = call(
        far_backward_kernel,
        (unit_qkv, far_probs, far_lse, crossed),
        jax.ShapeDtypeStruct((128, 48, 128), BF16),
        (units, pltpu.VMEM((3, 16, 128, 128), BF16)),
    )
    home = lax.all_to_all(back, SEQ, 0, 0, tiled=True)
    shape = jax.ShapeDtypeStruct((tokens, width), BF16)
    wide = jax.ShapeDtypeStruct((tokens, width), F32)
    attended, dq, dk, dv = call(
        band_backward_kernel,
        (query_rows, key_rows, value_rows, grad_rows, band_stats, crossed),
        (shape, wide, wide, wide),
        (units,),
    )
    grads = final_call((dq, dk, dv), home, shape)
    return (attended, *grads)


def solution(mesh):
    fine = Mesh(mesh.devices.reshape(4, 4, 4, 2, 4), ("x", "zl", "y", "core", "head"))
    rows = P(SEQ, "head")
    return jax.shard_map(
        program,
        mesh=fine,
        in_specs=(rows, rows, rows, rows, P("head", SEQ)),
        out_specs=(rows, rows, rows, rows),
        check_vma=False,
    )
```

```python
import jax
import jax.numpy as jnp
from jax import lax
from jax.experimental import pallas as pl
from jax.experimental.pallas import tpu as pltpu
from jax.sharding import Mesh
from jax.sharding import PartitionSpec as P

DH = 128
SCALING = DH ** (-0.5)
SENTINEL = -1e30
SEQ = ("x", "zl", "y", "core")
UNITS = 16
F32 = jnp.float32
BF16 = jnp.bfloat16


def nt(a, b):
    return lax.dot_general(a, b, (((1,), (1,)), ((), ())), preferred_element_type=F32)


def tn(a, b):
    return lax.dot_general(a, b, (((0,), (0,)), ((), ())), preferred_element_type=F32)


def nn(a, b):
    return lax.dot_general(a, b, (((1,), (0,)), ((), ())), preferred_element_type=F32)


def swap_matrix():
    rows = lax.broadcasted_iota(jnp.int32, (256, 256), 0)
    cols = lax.broadcasted_iota(jnp.int32, (256, 256), 1)
    return jnp.where(cols == (rows % 16) * 16 + rows // 16, 1.0, 0.0).astype(BF16)


def one_hot_rows(rows_n, cols_n, row, spread):
    rows = lax.broadcasted_iota(jnp.int32, (rows_n, cols_n), 0)
    cols = lax.broadcasted_iota(jnp.int32, (rows_n, cols_n), 1)
    hit = rows == cols * 8 + row if spread else cols == rows * 8 + row
    return jnp.where(hit, 1.0, 0.0).astype(BF16)


def split_rows(rows):
    hi = rows.astype(BF16).astype(F32)
    mid = (rows - hi).astype(BF16).astype(F32)
    low = (rows - hi - mid).astype(BF16).astype(F32)
    return jnp.concatenate([hi, mid, low, jnp.zeros_like(hi)], axis=0)


def join_rows(parts):
    return parts[0:32] + parts[32:64] + parts[64:96]


def stat_columns(stats):
    return jnp.transpose(split_rows(stats)).astype(BF16)


def take_stats(in_ref, base, row):
    collect = one_hot_rows(16, 128, row, False)
    pieces = []
    for block in range(8):
        rows = in_ref[block * 16 : block * 16 + 16, base : base + 8, :].reshape(128, 128)
        pieces.append(nn(collect, rows))
    return join_rows(jnp.transpose(jnp.concatenate(pieces, axis=0)))


def pack_rows(sources, out_ref):
    swap = swap_matrix()

    def step(block, carry):
        at = pl.multiple_of(block * 16, 16)
        for which, source in enumerate(sources):
            pieces = []
            for unit in range(UNITS):
                row, head = unit // 4, unit % 4
                pieces.append(
                    source[pl.ds(row * 128 + at, 16), head * 128 : head * 128 + 128]
                )
            moved = nn(swap, jnp.concatenate(pieces, axis=0)).astype(BF16)
            out_ref[pl.ds(at, 16), which * 16 : which * 16 + 16, :] = moved.reshape(
                16, 16, 128
            )
        return carry

    lax.fori_loop(0, 8, step, 0)


def pack_kernel(q_ref, k_ref, v_ref, out_ref):
    swap = swap_matrix()
    for block in range(2):
        place = slice(block * 16, block * 16 + 16)
        for which, source in enumerate((q_ref, k_ref, v_ref)):
            pieces = [
                source[unit // 4, place, (unit % 4) * 128 : (unit % 4) * 128 + 128]
                for unit in range(UNITS)
            ]
            moved = nn(swap, jnp.concatenate(pieces, axis=0)).astype(BF16)
            out_ref[place, which * 16 : which * 16 + 16, :] = moved.reshape(16, 16, 128)


def pack_call(arrays):
    rows = pl.BlockSpec((4, 32, arrays[0].shape[1]), lambda step: (0, step, 0))
    split = [array.reshape(4, 128, array.shape[1]) for array in arrays]
    return pl.pallas_call(
        pack_kernel,
        grid=(4,),
        out_shape=jax.ShapeDtypeStruct((128, 48, 128), BF16),
        in_specs=[rows] * 3,
        out_specs=pl.BlockSpec((32, 48, 128), lambda step: (step, 0, 0)),
        compiler_params=pltpu.CompilerParams(vmem_limit_bytes=16 * 1024 * 1024),
    )(*[pltpu.with_memory_space_constraint(array, pltpu.HBM) for array in split])


def masks(strict):
    keys = lax.broadcasted_iota(jnp.int32, (128, 128), 0)
    queries = lax.broadcasted_iota(jnp.int32, (128, 128), 1)
    return keys < queries if strict else keys <= queries


def forward_rows(q, k, visible):
    scores = nt(k, q) * SCALING
    top = jnp.max(jnp.where(visible, scores, SENTINEL), axis=0, keepdims=True)
    weights = jnp.where(visible, jnp.exp(scores - top), 0.0)
    total = jnp.sum(weights, axis=0, keepdims=True)
    return scores, top, weights, total


def far_forward_kernel(
    qkv_ref, unit_ref, probs_ref, out_ref, columns_ref, lse_ref, out_scr
):
    swap = swap_matrix()
    visible = masks(True)

    def unpack(block, carry):
        at = pl.multiple_of(block * 16, 16)
        for which in range(3):
            rows = qkv_ref[pl.ds(at, 16), which * 16 : which * 16 + 16, :].reshape(256, 128)
            unit_ref[which, :, pl.ds(at, 16), :] = (
                nn(swap, rows).astype(BF16).reshape(16, 16, 128)
            )
        return carry

    lax.fori_loop(0, 8, unpack, 0)
    lse_ref[...] = jnp.zeros((32, 128), F32)
    for unit in range(UNITS):
        q, k, v = unit_ref[0, unit], unit_ref[1, unit], unit_ref[2, unit]
        _, top, weights, total = forward_rows(q, k, visible)
        some = total > 0.0
        inverse = jnp.where(some, 1.0 / jnp.where(some, total, 1.0), 0.0)
        probs = weights * inverse
        probs_ref[unit] = probs
        out_scr[unit] = tn(probs.astype(BF16), v).astype(BF16)
        lse_ref[unit : unit + 1, :] = jnp.where(
            some, top + jnp.log(jnp.where(some, total, 1.0)), SENTINEL
        )

    def pack(block, carry):
        at = pl.multiple_of(block * 16, 16)
        rows = out_scr[:, pl.ds(at, 16), :].reshape(256, 128)
        out_ref[pl.ds(at, 16), :, :] = nn(swap, rows).astype(BF16).reshape(16, 16, 128)
        return carry

    lax.fori_loop(0, 8, pack, 0)
    columns_ref[...] = stat_columns(lse_ref[...])


def band_kernel(q_ref, k_ref, v_ref, g_ref, far_ref, columns_ref, out_ref, stats_ref):
    pack_rows((g_ref,), out_ref)
    out_ref[:, 16:32, :] = far_ref[...]
    visible = masks(False)

    for unit in range(UNITS):
        rows = slice((unit // 4) * 128, (unit // 4) * 128 + 128)
        cols = slice((unit % 4) * 128, (unit % 4) * 128 + 128)
        q, k, v, g = q_ref[rows, cols], k_ref[rows, cols], v_ref[rows, cols], g_ref[rows, cols]
        _, top, weights, total = forward_rows(q, k, visible)
        dot = jnp.sum(weights * nt(v, g), axis=0, keepdims=True)
        stats_ref[unit : unit + 1, :] = top + jnp.log(total)
        stats_ref[16 + unit : 17 + unit, :] = dot / total
    columns = stat_columns(stats_ref[...])
    home, away = one_hot_rows(128, 16, 0, True), one_hot_rows(128, 16, 1, True)
    for block in range(8):
        at = slice(block * 16, block * 16 + 16)
        rows = nn(home, columns[at]) + nn(away, columns_ref[at, :])
        out_ref[at, 32:40, :] = rows.astype(BF16).reshape(16, 8, 128)


def combine(band_lse, far_lse):
    highest = jnp.maximum(band_lse, far_lse)
    band_part = jnp.exp(band_lse - highest)
    far_part = jnp.exp(far_lse - highest)
    norm = band_part + far_part
    return highest + jnp.log(norm), band_part / norm, far_part / norm


def far_backward_kernel(unit_ref, probs_ref, lse_ref, g_ref, out_ref, g_scr, out_scr):
    swap = swap_matrix()

    def unpack(block, carry):
        at = pl.multiple_of(block * 16, 16)
        rows = g_ref[pl.ds(at, 16), 0:16, :].reshape(256, 128)
        g_scr[:, pl.ds(at, 16), :] = nn(swap, rows).astype(BF16).reshape(16, 16, 128)
        return carry

    lax.fori_loop(0, 8, unpack, 0)
    band = take_stats(g_ref, 32, 0)
    _, band_share, far_share = combine(band[0:16], lse_ref[0:16, :])
    band_delta = band_share * band[16:32]
    for unit in range(UNITS):
        q, k, v, g = unit_ref[0, unit], unit_ref[1, unit], unit_ref[2, unit], g_scr[unit]
        probs = probs_ref[unit] * far_share[unit : unit + 1]
        dprob = nt(v, g)
        delta = band_delta[unit : unit + 1] + jnp.sum(probs * dprob, axis=0, keepdims=True)
        dscore = (probs * (dprob - delta)).astype(BF16)
        out_scr[0, unit] = (tn(dscore, k) * SCALING).astype(BF16)
        out_scr[1, unit] = (nn(dscore, q) * SCALING).astype(BF16)
        out_scr[2, unit] = nn(probs.astype(BF16), g).astype(BF16)

    def pack(block, carry):
        at = pl.multiple_of(block * 16, 16)
        for which in range(3):
            rows = out_scr[which, :, pl.ds(at, 16), :].reshape(256, 128)
            out_ref[pl.ds(at, 16), which * 16 : which * 16 + 16, :] = (
                nn(swap, rows).astype(BF16).reshape(16, 16, 128)
            )
        return carry

    lax.fori_loop(0, 8, pack, 0)


def band_backward_kernel(
    q_ref, k_ref, v_ref, g_ref, band_ref, far_ref, att_ref, dq_ref, dk_ref, dv_ref, far_scr
):
    swap = swap_matrix()
    visible = masks(False)

    def unpack(block, carry):
        at = pl.multiple_of(block * 16, 16)
        rows = far_ref[pl.ds(at, 16), 16:32, :].reshape(256, 128)
        far_scr[:, pl.ds(at, 16), :] = nn(swap, rows).astype(BF16).reshape(16, 16, 128)
        return carry

    lax.fori_loop(0, 8, unpack, 0)
    far_lse = take_stats(far_ref, 32, 1)[0:16]
    lse, band_share, far_share = combine(band_ref[0:16, :], far_lse)
    band_delta = band_share * band_ref[16:32, :]
    shares = jnp.transpose(
        jnp.concatenate([far_share, jnp.zeros((112, 128), F32)], axis=0)
    )
    ones = jnp.ones((8, 128), BF16)
    for unit in range(UNITS):
        rows = slice((unit // 4) * 128, (unit // 4) * 128 + 128)
        cols = slice((unit % 4) * 128, (unit % 4) * 128 + 128)
        q, k, v, g = q_ref[rows, cols], k_ref[rows, cols], v_ref[rows, cols], g_ref[rows, cols]
        out_far = far_scr[unit].astype(F32)
        product = g.astype(F32) * out_far
        high = product.astype(BF16)
        low = (product - high.astype(F32)).astype(BF16)
        dot_far = (nt(ones, high) + nt(ones, low))[0:1]
        delta = band_delta[unit : unit + 1] + far_share[unit : unit + 1] * dot_far
        scores = nt(k, q) * SCALING
        probs = jnp.where(visible, jnp.exp(scores - lse[unit : unit + 1]), 0.0)
        rounded = probs.astype(BF16)
        dscore = (probs * (nt(v, g) - delta)).astype(BF16)
        att_ref[rows, cols] = (tn(rounded, v) + shares[:, unit : unit + 1] * out_far).astype(BF16)
        dq_ref[rows, cols] = tn(dscore, k) * SCALING
        dk_ref[rows, cols] = nn(dscore, q) * SCALING
        dv_ref[rows, cols] = nn(rounded, g)


def final_kernel(dq_ref, dk_ref, dv_ref, far_ref, query_ref, key_ref, value_ref):
    bands, outs = (dq_ref, dk_ref, dv_ref), (query_ref, key_ref, value_ref)
    rows = lax.broadcasted_iota(jnp.int32, (64, 256), 0)
    cols = lax.broadcasted_iota(jnp.int32, (64, 256), 1)
    source = (rows % 16) * 16 + pl.program_id(0) * 4 + rows // 16
    choose = jnp.where(cols == source, 1.0, 0.0).astype(BF16)
    for block in range(8):
        place = slice(block * 16, block * 16 + 16)
        for which in range(3):
            far = far_ref[place, which * 16 : which * 16 + 16, :].reshape(256, 128)
            moved = nn(choose, far)
            for head in range(4):
                at = slice(head * 128, head * 128 + 128)
                piece = moved[head * 16 : head * 16 + 16]
                outs[which][place, at] = (bands[which][place, at] + piece).astype(BF16)


def final_call(bands, home, shape):
    rows = pl.BlockSpec((128, shape.shape[1]), lambda step: (step, 0))
    whole = pl.BlockSpec(home.shape, lambda step: (0, 0, 0))
    return pl.pallas_call(
        final_kernel,
        grid=(4,),
        out_shape=(shape,) * 3,
        in_specs=[rows] * 3 + [whole],
        out_specs=(rows,) * 3,
        compiler_params=pltpu.CompilerParams(vmem_limit_bytes=16 * 1024 * 1024),
    )(*[pltpu.with_memory_space_constraint(band, pltpu.HBM) for band in bands], home)


def call(kernel, args, outs, scratch=()):
    vmem = pl.BlockSpec(memory_space=pltpu.VMEM)
    single = not isinstance(outs, tuple)
    return pl.pallas_call(
        kernel,
        out_shape=outs,
        in_specs=[vmem] * len(args),
        out_specs=vmem if single else tuple([vmem] * len(outs)),
        scratch_shapes=list(scratch),
        compiler_params=pltpu.CompilerParams(vmem_limit_bytes=24 * 1024 * 1024),
    )(*args)


def shifted(values, axis, by):
    return lax.ppermute(values, axis, [(i, (i + by) % 4) for i in range(4)])


def around(values, axis):
    return jnp.concatenate(
        [values] + [shifted(values, axis, by) for by in (1, 2, 3)], axis=0
    )


def column_order(width):
    zl, y, core = lax.axis_index("zl"), lax.axis_index("y"), lax.axis_index("core")
    rows = lax.broadcasted_iota(jnp.int32, (width, width), 0)
    cols = lax.broadcasted_iota(jnp.int32, (width, width), 1)
    core_at = (cols // 512 + core) % 2
    y_at = (y - (cols // 128) % 4 + 4) % 4
    zl_at = (zl - (cols // 32) % 4 + 4) % 4
    source = zl_at * 256 + y_at * 64 + core_at * 32 + cols % 32
    return (rows == source).astype(BF16)


def program(query_rows, key_rows, value_rows, out_grad, out_weight):
    tokens, width = query_rows.shape
    x, head = lax.axis_index("x"), lax.axis_index("head")

    sent = pack_call((query_rows, key_rows, value_rows))
    own = out_weight.T
    weight = lax.ppermute(
        own,
        ("x", "head"),
        [(a * 4 + h, h * 4 + a) for a in range(4) for h in range(4)],
    )
    weight = around(around(weight, "zl"), "y")
    mine = jnp.stack([weight] + [shifted(weight, "x", by) for by in (1, 2, 3)])
    far_qkv = lax.all_to_all(sent, SEQ, 0, 0, tiled=True)
    others = lax.ppermute(mine, "core", [(0, 1), (1, 0)])
    ordered = jnp.dot(out_grad, column_order(out_grad.shape[1]), preferred_element_type=F32)
    ordered = ordered.astype(BF16)

    def partial(target, mine, others):
        at = (x - target + 8) % 4
        near = lax.dynamic_index_in_dim(mine, at, 0, keepdims=False)
        other = lax.dynamic_index_in_dim(others, at, 0, keepdims=False)
        return jnp.dot(ordered[:, :512], near, preferred_element_type=F32) + jnp.dot(
            ordered[:, 512:], other, preferred_element_type=F32
        )

    middle = tokens // 2
    low, high = slice(0, middle), slice(middle, tokens)

    opposite = partial(head + 2, mine, others).astype(BF16)
    opposite, mine, others = lax.optimization_barrier((opposite, mine, others))
    above, below, here = (partial(head + by, mine, others) for by in (1, -1, 0))
    far_up = shifted(opposite[low], "head", 1)
    far_down = shifted(opposite[high], "head", -1)
    near_up = shifted(above[high].astype(BF16), "head", 1)
    near_down = shifted(below[low].astype(BF16), "head", -1)
    last_up = shifted((far_up.astype(F32) + above[low]).astype(BF16), "head", 1)
    last_down = shifted(
        (far_down.astype(F32) + below[high]).astype(BF16), "head", -1
    )

    stats = jax.ShapeDtypeStruct((32, 128), F32)
    units = pltpu.VMEM((16, 128, 128), BF16)
    unit_qkv, far_probs, far_out, far_columns, far_lse = call(
        far_forward_kernel,
        (far_qkv,),
        (
            jax.ShapeDtypeStruct((3, 16, 128, 128), BF16),
            jax.ShapeDtypeStruct((16, 128, 128), F32),
            jax.ShapeDtypeStruct((128, 16, 128), BF16),
            jax.ShapeDtypeStruct((128, 128), BF16),
            stats,
        ),
        (units,),
    )
    last_up, last_down, far_out = lax.optimization_barrier(
        (last_up, last_down, far_out)
    )
    grad_rows = jnp.concatenate(
        [
            (
                here[low] + near_down.astype(F32) + last_up.astype(F32)
            ).astype(BF16),
            (
                here[high] + near_up.astype(F32) + last_down.astype(F32)
            ).astype(BF16),
        ],
        axis=0,
    )

    sent_grad, band_stats = call(
        band_kernel,
        (query_rows, key_rows, value_rows, grad_rows, far_out, far_columns),
        (jax.ShapeDtypeStruct((128, 40, 128), BF16), stats),
    )
    crossed = lax.all_to_all(sent_grad, SEQ, 0, 0, tiled=True)
    back = call(
        far_backward_kernel,
        (unit_qkv, far_probs, far_lse, crossed),
        jax.ShapeDtypeStruct((128, 48, 128), BF16),
        (units, pltpu.VMEM((3, 16, 128, 128), BF16)),
    )
    home = lax.all_to_all(back, SEQ, 0, 0, tiled=True)
    shape = jax.ShapeDtypeStruct((tokens, width), BF16)
    wide = jax.ShapeDtypeStruct((tokens, width), F32)
    attended, dq, dk, dv = call(
        band_backward_kernel,
        (query_rows, key_rows, value_rows, grad_rows, band_stats, crossed),
        (shape, wide, wide, wide),
        (units,),
    )
    grads = final_call((dq, dk, dv), home, shape)
    return (attended, *grads)


def solution(mesh):
    fine = Mesh(mesh.devices.reshape(4, 4, 4, 2, 4), ("x", "zl", "y", "core", "head"))
    rows = P(SEQ, "head")
    return jax.shard_map(
        program,
        mesh=fine,
        in_specs=(rows, rows, rows, rows, P("head", SEQ)),
        out_specs=(rows, rows, rows, rows),
        check_vma=False,
    )
```

```python
import jax
import jax.numpy as jnp
from jax import lax
from jax.experimental import pallas as pl
from jax.experimental.pallas import tpu as pltpu
from jax.sharding import Mesh
from jax.sharding import PartitionSpec as P

DH = 128
SCALING = DH ** (-0.5)
SENTINEL = -1e30
SEQ = ("x", "zl", "y", "core")
UNITS = 16
F32 = jnp.float32
BF16 = jnp.bfloat16


def nt(a, b):
    return lax.dot_general(a, b, (((1,), (1,)), ((), ())), preferred_element_type=F32)


def tn(a, b):
    return lax.dot_general(a, b, (((0,), (0,)), ((), ())), preferred_element_type=F32)


def nn(a, b):
    return lax.dot_general(a, b, (((1,), (0,)), ((), ())), preferred_element_type=F32)


def swap_matrix():
    rows = lax.broadcasted_iota(jnp.int32, (256, 256), 0)
    cols = lax.broadcasted_iota(jnp.int32, (256, 256), 1)
    return jnp.where(cols == (rows % 16) * 16 + rows // 16, 1.0, 0.0).astype(BF16)


def one_hot_rows(rows_n, cols_n, row, spread):
    rows = lax.broadcasted_iota(jnp.int32, (rows_n, cols_n), 0)
    cols = lax.broadcasted_iota(jnp.int32, (rows_n, cols_n), 1)
    hit = rows == cols * 8 + row if spread else cols == rows * 8 + row
    return jnp.where(hit, 1.0, 0.0).astype(BF16)


def split_rows(rows):
    hi = rows.astype(BF16).astype(F32)
    mid = (rows - hi).astype(BF16).astype(F32)
    low = (rows - hi - mid).astype(BF16).astype(F32)
    return jnp.concatenate([hi, mid, low, jnp.zeros_like(hi)], axis=0)


def join_rows(parts):
    return parts[0:32] + parts[32:64] + parts[64:96]


def stat_columns(stats):
    return jnp.transpose(split_rows(stats)).astype(BF16)


def take_stats(in_ref, base, row):
    collect = one_hot_rows(16, 128, row, False)
    pieces = []
    for block in range(8):
        rows = in_ref[block * 16 : block * 16 + 16, base : base + 8, :].reshape(128, 128)
        pieces.append(nn(collect, rows))
    return join_rows(jnp.transpose(jnp.concatenate(pieces, axis=0)))


def pack_rows(sources, out_ref):
    swap = swap_matrix()

    def step(block, carry):
        at = pl.multiple_of(block * 16, 16)
        for which, source in enumerate(sources):
            pieces = []
            for unit in range(UNITS):
                row, head = unit // 4, unit % 4
                pieces.append(
                    source[pl.ds(row * 128 + at, 16), head * 128 : head * 128 + 128]
                )
            moved = nn(swap, jnp.concatenate(pieces, axis=0)).astype(BF16)
            out_ref[pl.ds(at, 16), which * 16 : which * 16 + 16, :] = moved.reshape(
                16, 16, 128
            )
        return carry

    lax.fori_loop(0, 8, step, 0)


def pack_kernel(q_ref, k_ref, v_ref, out_ref):
    swap = swap_matrix()
    for block in range(2):
        place = slice(block * 16, block * 16 + 16)
        for which, source in enumerate((q_ref, k_ref, v_ref)):
            pieces = [
                source[unit // 4, place, (unit % 4) * 128 : (unit % 4) * 128 + 128]
                for unit in range(UNITS)
            ]
            moved = nn(swap, jnp.concatenate(pieces, axis=0)).astype(BF16)
            out_ref[place, which * 16 : which * 16 + 16, :] = moved.reshape(16, 16, 128)


def pack_call(arrays):
    rows = pl.BlockSpec((4, 32, arrays[0].shape[1]), lambda step: (0, step, 0))
    split = [array.reshape(4, 128, array.shape[1]) for array in arrays]
    return pl.pallas_call(
        pack_kernel,
        grid=(4,),
        out_shape=jax.ShapeDtypeStruct((128, 48, 128), BF16),
        in_specs=[rows] * 3,
        out_specs=pl.BlockSpec((32, 48, 128), lambda step: (step, 0, 0)),
        compiler_params=pltpu.CompilerParams(vmem_limit_bytes=16 * 1024 * 1024),
    )(*[pltpu.with_memory_space_constraint(array, pltpu.HBM) for array in split])


def masks(strict):
    keys = lax.broadcasted_iota(jnp.int32, (128, 128), 0)
    queries = lax.broadcasted_iota(jnp.int32, (128, 128), 1)
    return keys < queries if strict else keys <= queries


def forward_rows(q, k, visible):
    scores = nt(k, q) * SCALING
    top = jnp.max(jnp.where(visible, scores, SENTINEL), axis=0, keepdims=True)
    weights = jnp.where(visible, jnp.exp(scores - top), 0.0)
    total = jnp.sum(weights, axis=0, keepdims=True)
    return scores, top, weights, total


def far_forward_kernel(
    qkv_ref, unit_ref, probs_ref, out_ref, columns_ref, lse_ref, out_scr
):
    swap = swap_matrix()
    visible = masks(True)

    def unpack(block, carry):
        at = pl.multiple_of(block * 16, 16)
        for which in range(3):
            rows = qkv_ref[pl.ds(at, 16), which * 16 : which * 16 + 16, :].reshape(256, 128)
            unit_ref[which, :, pl.ds(at, 16), :] = (
                nn(swap, rows).astype(BF16).reshape(16, 16, 128)
            )
        return carry

    lax.fori_loop(0, 8, unpack, 0)
    lse_ref[...] = jnp.zeros((32, 128), F32)
    for unit in range(UNITS):
        q, k, v = unit_ref[0, unit], unit_ref[1, unit], unit_ref[2, unit]
        _, top, weights, total = forward_rows(q, k, visible)
        some = total > 0.0
        inverse = jnp.where(some, 1.0 / jnp.where(some, total, 1.0), 0.0)
        probs = weights * inverse
        probs_ref[unit] = probs
        out_scr[unit] = tn(probs.astype(BF16), v).astype(BF16)
        lse_ref[unit : unit + 1, :] = jnp.where(
            some, top + jnp.log(jnp.where(some, total, 1.0)), SENTINEL
        )

    def pack(block, carry):
        at = pl.multiple_of(block * 16, 16)
        rows = out_scr[:, pl.ds(at, 16), :].reshape(256, 128)
        out_ref[pl.ds(at, 16), :, :] = nn(swap, rows).astype(BF16).reshape(16, 16, 128)
        return carry

    lax.fori_loop(0, 8, pack, 0)
    columns_ref[...] = stat_columns(lse_ref[...])


def band_kernel(q_ref, k_ref, v_ref, g_ref, far_ref, columns_ref, out_ref, stats_ref):
    pack_rows((g_ref,), out_ref)
    out_ref[:, 16:32, :] = far_ref[...]
    visible = masks(False)

    for unit in range(UNITS):
        rows = slice((unit // 4) * 128, (unit // 4) * 128 + 128)
        cols = slice((unit % 4) * 128, (unit % 4) * 128 + 128)
        q, k, v, g = q_ref[rows, cols], k_ref[rows, cols], v_ref[rows, cols], g_ref[rows, cols]
        _, top, weights, total = forward_rows(q, k, visible)
        dot = jnp.sum(weights * nt(v, g), axis=0, keepdims=True)
        stats_ref[unit : unit + 1, :] = top + jnp.log(total)
        stats_ref[16 + unit : 17 + unit, :] = dot / total
    columns = stat_columns(stats_ref[...])
    home, away = one_hot_rows(128, 16, 0, True), one_hot_rows(128, 16, 1, True)
    for block in range(8):
        at = slice(block * 16, block * 16 + 16)
        rows = nn(home, columns[at]) + nn(away, columns_ref[at, :])
        out_ref[at, 32:40, :] = rows.astype(BF16).reshape(16, 8, 128)


def combine(band_lse, far_lse):
    highest = jnp.maximum(band_lse, far_lse)
    band_part = jnp.exp(band_lse - highest)
    far_part = jnp.exp(far_lse - highest)
    norm = band_part + far_part
    return highest + jnp.log(norm), band_part / norm, far_part / norm


def far_backward_kernel(unit_ref, probs_ref, lse_ref, g_ref, out_ref, g_scr, out_scr):
    swap = swap_matrix()

    def unpack(block, carry):
        at = pl.multiple_of(block * 16, 16)
        rows = g_ref[pl.ds(at, 16), 0:16, :].reshape(256, 128)
        g_scr[:, pl.ds(at, 16), :] = nn(swap, rows).astype(BF16).reshape(16, 16, 128)
        return carry

    lax.fori_loop(0, 8, unpack, 0)
    band = take_stats(g_ref, 32, 0)
    _, band_share, far_share = combine(band[0:16], lse_ref[0:16, :])
    band_delta = band_share * band[16:32]
    for unit in range(UNITS):
        q, k, v, g = unit_ref[0, unit], unit_ref[1, unit], unit_ref[2, unit], g_scr[unit]
        probs = probs_ref[unit] * far_share[unit : unit + 1]
        dprob = nt(v, g)
        delta = band_delta[unit : unit + 1] + jnp.sum(probs * dprob, axis=0, keepdims=True)
        dscore = (probs * (dprob - delta)).astype(BF16)
        out_scr[0, unit] = (tn(dscore, k) * SCALING).astype(BF16)
        out_scr[1, unit] = (nn(dscore, q) * SCALING).astype(BF16)
        out_scr[2, unit] = nn(probs.astype(BF16), g).astype(BF16)

    def pack(block, carry):
        at = pl.multiple_of(block * 16, 16)
        for which in range(3):
            rows = out_scr[which, :, pl.ds(at, 16), :].reshape(256, 128)
            out_ref[pl.ds(at, 16), which * 16 : which * 16 + 16, :] = (
                nn(swap, rows).astype(BF16).reshape(16, 16, 128)
            )
        return carry

    lax.fori_loop(0, 8, pack, 0)


def band_backward_kernel(
    q_ref, k_ref, v_ref, g_ref, band_ref, far_ref, att_ref, dq_ref, dk_ref, dv_ref, far_scr
):
    swap = swap_matrix()
    visible = masks(False)

    def unpack(block, carry):
        at = pl.multiple_of(block * 16, 16)
        rows = far_ref[pl.ds(at, 16), 16:32, :].reshape(256, 128)
        far_scr[:, pl.ds(at, 16), :] = nn(swap, rows).astype(BF16).reshape(16, 16, 128)
        return carry

    lax.fori_loop(0, 8, unpack, 0)
    far_lse = take_stats(far_ref, 32, 1)[0:16]
    lse, band_share, far_share = combine(band_ref[0:16, :], far_lse)
    band_delta = band_share * band_ref[16:32, :]
    shares = jnp.transpose(
        jnp.concatenate([far_share, jnp.zeros((112, 128), F32)], axis=0)
    )
    ones = jnp.ones((8, 128), BF16)
    for unit in range(UNITS):
        rows = slice((unit // 4) * 128, (unit // 4) * 128 + 128)
        cols = slice((unit % 4) * 128, (unit % 4) * 128 + 128)
        q, k, v, g = q_ref[rows, cols], k_ref[rows, cols], v_ref[rows, cols], g_ref[rows, cols]
        out_far = far_scr[unit].astype(F32)
        product = g.astype(F32) * out_far
        high = product.astype(BF16)
        low = (product - high.astype(F32)).astype(BF16)
        dot_far = (nt(ones, high) + nt(ones, low))[0:1]
        delta = band_delta[unit : unit + 1] + far_share[unit : unit + 1] * dot_far
        scores = nt(k, q) * SCALING
        probs = jnp.where(visible, jnp.exp(scores - lse[unit : unit + 1]), 0.0)
        rounded = probs.astype(BF16)
        dscore = (probs * (nt(v, g) - delta)).astype(BF16)
        att_ref[rows, cols] = (tn(rounded, v) + shares[:, unit : unit + 1] * out_far).astype(BF16)
        dq_ref[rows, cols] = tn(dscore, k) * SCALING
        dk_ref[rows, cols] = nn(dscore, q) * SCALING
        dv_ref[rows, cols] = nn(rounded, g)


def final_kernel(dq_ref, dk_ref, dv_ref, far_ref, query_ref, key_ref, value_ref):
    bands, outs = (dq_ref, dk_ref, dv_ref), (query_ref, key_ref, value_ref)
    rows = lax.broadcasted_iota(jnp.int32, (64, 256), 0)
    cols = lax.broadcasted_iota(jnp.int32, (64, 256), 1)
    source = (rows % 16) * 16 + pl.program_id(0) * 4 + rows // 16
    choose = jnp.where(cols == source, 1.0, 0.0).astype(BF16)
    for block in range(8):
        place = slice(block * 16, block * 16 + 16)
        for which in range(3):
            far = far_ref[place, which * 16 : which * 16 + 16, :].reshape(256, 128)
            moved = nn(choose, far)
            for head in range(4):
                at = slice(head * 128, head * 128 + 128)
                piece = moved[head * 16 : head * 16 + 16]
                outs[which][place, at] = (bands[which][place, at] + piece).astype(BF16)


def final_call(bands, home, shape):
    rows = pl.BlockSpec((128, shape.shape[1]), lambda step: (step, 0))
    whole = pl.BlockSpec(home.shape, lambda step: (0, 0, 0))
    return pl.pallas_call(
        final_kernel,
        grid=(4,),
        out_shape=(shape,) * 3,
        in_specs=[rows] * 3 + [whole],
        out_specs=(rows,) * 3,
        compiler_params=pltpu.CompilerParams(vmem_limit_bytes=16 * 1024 * 1024),
    )(*[pltpu.with_memory_space_constraint(band, pltpu.HBM) for band in bands], home)


def call(kernel, args, outs, scratch=()):
    vmem = pl.BlockSpec(memory_space=pltpu.VMEM)
    single = not isinstance(outs, tuple)
    return pl.pallas_call(
        kernel,
        out_shape=outs,
        in_specs=[vmem] * len(args),
        out_specs=vmem if single else tuple([vmem] * len(outs)),
        scratch_shapes=list(scratch),
        compiler_params=pltpu.CompilerParams(vmem_limit_bytes=24 * 1024 * 1024),
    )(*args)


def shifted(values, axis, by):
    return lax.ppermute(values, axis, [(i, (i + by) % 4) for i in range(4)])


def around(values, axis):
    return jnp.concatenate(
        [values] + [shifted(values, axis, by) for by in (1, 2, 3)], axis=0
    )


def column_order(width):
    zl, y, core = lax.axis_index("zl"), lax.axis_index("y"), lax.axis_index("core")
    rows = lax.broadcasted_iota(jnp.int32, (width, width), 0)
    cols = lax.broadcasted_iota(jnp.int32, (width, width), 1)
    core_at = (cols // 512 + core) % 2
    y_at = (y - (cols // 128) % 4 + 4) % 4
    zl_at = (zl - (cols // 32) % 4 + 4) % 4
    source = zl_at * 256 + y_at * 64 + core_at * 32 + cols % 32
    return (rows == source).astype(BF16)


def program(query_rows, key_rows, value_rows, out_grad, out_weight):
    tokens, width = query_rows.shape
    x, head = lax.axis_index("x"), lax.axis_index("head")

    sent = pack_call((query_rows, key_rows, value_rows))
    own = out_weight.T
    weight = lax.ppermute(
        own,
        ("x", "head"),
        [(a * 4 + h, h * 4 + a) for a in range(4) for h in range(4)],
    )
    weight = around(around(weight, "zl"), "y")
    mine = jnp.stack([weight] + [shifted(weight, "x", by) for by in (1, 2, 3)])
    far_qkv = lax.all_to_all(sent, SEQ, 0, 0, tiled=True)
    others = lax.ppermute(mine, "core", [(0, 1), (1, 0)])
    ordered = jnp.dot(out_grad, column_order(out_grad.shape[1]), preferred_element_type=F32)
    ordered = ordered.astype(BF16)

    def partial(target, mine, others):
        at = (x - target + 8) % 4
        near = lax.dynamic_index_in_dim(mine, at, 0, keepdims=False)
        other = lax.dynamic_index_in_dim(others, at, 0, keepdims=False)
        return jnp.dot(ordered[:, :512], near, preferred_element_type=F32) + jnp.dot(
            ordered[:, 512:], other, preferred_element_type=F32
        )

    middle = tokens // 2
    low, high = slice(0, middle), slice(middle, tokens)

    opposite = partial(head + 2, mine, others).astype(BF16)
    opposite, mine, others = lax.optimization_barrier((opposite, mine, others))
    above, below, here = (partial(head + by, mine, others) for by in (1, -1, 0))
    far_up = shifted(opposite[low], "head", 1)
    far_down = shifted(opposite[high], "head", -1)
    last_up = shifted((far_up.astype(F32) + above[low]).astype(BF16), "head", 1)
    last_down = shifted(
        (far_down.astype(F32) + below[high]).astype(BF16), "head", -1
    )

    stats = jax.ShapeDtypeStruct((32, 128), F32)
    units = pltpu.VMEM((16, 128, 128), BF16)
    near_high, near_low, far_qkv = lax.optimization_barrier(
        (above[high].astype(BF16), below[low].astype(BF16), far_qkv)
    )
    near_up = shifted(near_high, "head", 1)
    near_down = shifted(near_low, "head", -1)
    unit_qkv, far_probs, far_out, far_columns, far_lse = call(
        far_forward_kernel,
        (far_qkv,),
        (
            jax.ShapeDtypeStruct((3, 16, 128, 128), BF16),
            jax.ShapeDtypeStruct((16, 128, 128), F32),
            jax.ShapeDtypeStruct((128, 16, 128), BF16),
            jax.ShapeDtypeStruct((128, 128), BF16),
            stats,
        ),
        (units,),
    )
    last_up, last_down, far_out = lax.optimization_barrier(
        (last_up, last_down, far_out)
    )
    grad_rows = jnp.concatenate(
        [
            (
                here[low] + near_down.astype(F32) + last_up.astype(F32)
            ).astype(BF16),
            (
                here[high] + near_up.astype(F32) + last_down.astype(F32)
            ).astype(BF16),
        ],
        axis=0,
    )

    sent_grad, band_stats = call(
        band_kernel,
        (query_rows, key_rows, value_rows, grad_rows, far_out, far_columns),
        (jax.ShapeDtypeStruct((128, 40, 128), BF16), stats),
    )
    crossed = lax.all_to_all(sent_grad, SEQ, 0, 0, tiled=True)
    back = call(
        far_backward_kernel,
        (unit_qkv, far_probs, far_lse, crossed),
        jax.ShapeDtypeStruct((128, 48, 128), BF16),
        (units, pltpu.VMEM((3, 16, 128, 128), BF16)),
    )
    home = lax.all_to_all(back, SEQ, 0, 0, tiled=True)
    shape = jax.ShapeDtypeStruct((tokens, width), BF16)
    wide = jax.ShapeDtypeStruct((tokens, width), F32)
    attended, dq, dk, dv = call(
        band_backward_kernel,
        (query_rows, key_rows, value_rows, grad_rows, band_stats, crossed),
        (shape, wide, wide, wide),
        (units,),
    )
    grads = final_call((dq, dk, dv), home, shape)
    return (attended, *grads)


def solution(mesh):
    fine = Mesh(mesh.devices.reshape(4, 4, 4, 2, 4), ("x", "zl", "y", "core", "head"))
    rows = P(SEQ, "head")
    return jax.shard_map(
        program,
        mesh=fine,
        in_specs=(rows, rows, rows, rows, P("head", SEQ)),
        out_specs=(rows, rows, rows, rows),
        check_vma=False,
    )
```
